32 devices in a mesh: gx: 4 (over z), gy: 2 (over y), gz: 4 (over x, core).
Axes of the slice: x: 2, y: 2, z: 4, core: 2. Of those that a mesh axis runs over, the one named last changes fastest.
Arguments:
- adjoint_guess: float32 [2, 20, 128, 1024], P(None, 'gz', 'gy', 'gx'), may hold values from -6 to 6
- viscosity: float32 [20, 128, 1024], P('gz', 'gy', 'gx'), may hold values from 0.2 to 2
- friction: float32 [128, 1024], P('gy', 'gx'), may hold values from 0.2 to 5
- base_velocity: float32 [2, 128, 1024], P(None, 'gy', 'gx'), may hold values from -6 to 6
- surface_slope: float32 [2, 128, 1024], P(None, 'gy', 'gx'), may hold values from -6 to 6
- ice_mask: int32 [128, 1024], P('gy', 'gx'), may hold values 0 or 1
- pixel_misfit: float32 [524288], P(('gx', 'gy', 'gz')), may hold values from -6 to 6
- pixel_look: float32 [524288], P(('gx', 'gy', 'gz')), may hold values from -3.140625 to 3.140625
- pixel_tile: int32 [524288, 1], P(('gx', 'gy', 'gz')), may hold values from 0 to 7; in each aligned block of 16384 rows (0 to 16383, 16384 to 32767, ...) at most 4096 rows name the same one
- pixel_cell: int32 [524288], P(('gx', 'gy', 'gz')), may hold values from 0 to 16383
- pixel_count: int32 [32], P(('gx', 'gy', 'gz')), may hold values from 1 to 16384, 393216 in all
Outputs:
- adjoint: float32 [2, 20, 128, 1024], P(None, 'gz', 'gy', 'gx')
- sensitivity_maps: float32 [2, 128, 1024], P(None, ('gy', 'gz'), 'gx')
The draws below stay inside these ranges and needn't reach their ends.
Inputs may be any that keep to these rules, and one draw needn't show every extreme that they name: `pixel_tile`: among the rows of one device no tile is named more than 4096 times, a bound that some block reaches. `pixel_count`: rows of a device from its count on are padding.
All inputs are finite; a program needn't handle non-finite values. No bound on the sum of `ice_mask` on one device may be relied on, other than what follows from the above.
Results may differ from the reference program's by a relative error of at most 0.00002.
Values sent between devices are 32-bit elements; how exact they have to be, the bound alone decides.
A program may use at most 128 MiB of HBM per device.

```python
import math
import jax
import jax.numpy as jnp
import numpy as np

CX = 256
CY = 64
ITERS = 2
ROWS_DEV = 16384
L = 20
NX = 1024
NY = 128
TILES = 8
CAP = 4096
ROWS = 524288
N_GX = 4
N_GY = 2
N_GZ = 4


def plant(array, rng, low, top_value):
    shape = array.shape
    spot = [jax.random.randint(jax.random.fold_in(rng, axis), (), 0, shape[axis]) for axis in range(len(shape))]
    array = array.at[tuple(spot)].set(low)
    longest = shape.index(max(shape))
    spot[longest] = (spot[longest] + 1) % shape[longest]
    return array.at[tuple(spot)].set(top_value)


def levels(own_key, extent, cuts, low, high):
    factor_of = 1.0
    for dim, blocks in cuts:
        steps = jax.random.uniform(jax.random.fold_in(jax.random.fold_in(own_key, 6), dim), (blocks,), jnp.float32, low / len(cuts), high / len(cuts))
        factor_of = factor_of * jnp.repeat(jnp.exp(steps), extent[dim] // blocks).reshape((-1,) + (1,) * (len(extent) - 1 - dim))
    return factor_of


def split_up(amount, total, limit, skew):
    loads = [(1 << 20) // math.isqrt(grade ** skew) + 1 for grade in range(2, amount + 1)]
    spare, holding = total - limit - (amount - 1), [1] * (amount - 1)
    while spare > 0:
        candidates = [i for i in range(amount - 1) if holding[i] < limit]
        whole, left = sum([loads[i] for i in candidates]), spare
        for i in candidates:
            addition = min(limit - holding[i], max(1, left * loads[i] // whole), spare)
            holding[i] = holding[i] + addition
            spare = spare - addition
    return np.array([limit] + holding)


def ragged_sizes(key, amount, total, most, lean):
    if amount == 2:
        one = jax.random.randint(key, (), max(1, total - most), min(most, total - 1) + 1)
        return jnp.stack([one, total - one])
    sizes = jnp.asarray(split_up(amount, total, most, lean), jnp.int32)
    twos = (amount - 1) // 2
    source_of, sink = sizes[1:1 + 2 * twos:2], sizes[2:2 + 2 * twos:2]
    slack = jnp.minimum(source_of - 1, most - sink)
    passed = jax.random.randint(jax.random.fold_in(key, 1), (twos,), 0, 1 << 20) % (slack + 1)
    sizes = sizes.at[1:1 + 2 * twos:2].set(source_of - passed).at[2:2 + 2 * twos:2].set(sink + passed)
    return sizes[jax.random.permutation(jax.random.fold_in(key, 2), amount)]


def assign_block(own_key, own, number, rows, amount, top, bound, slope):
    sequence = jax.random.permutation(own_key, amount)
    heavy_load, usual = load_shares(amount, rows * top, bound, slope, True), load_shares(amount, rows * top, bound, slope, False)
    places = jnp.arange(amount)

    def named(tallies, turn):
        used = int((tallies > 0).sum())
        fixed = max(1, used // 4)
        moved = fixed + (places - fixed + turn * (used - fixed)) % max(1, amount - fixed)
        return jnp.zeros((amount,), jnp.int32).at[sequence[jnp.where(places < fixed, places, moved)]].set(jnp.asarray(tallies, jnp.int32))

    tallies = jnp.where(number % 4 == 0, named(heavy_load, number // 4), named(usual, number - number // 4 - 1))
    mixed = jax.random.permutation(jax.random.fold_in(own, 3), amount)
    donor, taker = mixed[0:amount // 2 * 2:2], mixed[1:amount // 2 * 2:2]
    slack = jnp.minimum(tallies[donor] - 1, bound - tallies[taker]) // 2
    slack = jnp.where((donor == sequence[0]) | (taker == sequence[0]) | (tallies[taker] == 0), 0, jnp.maximum(slack, 0))
    moved = jax.random.randint(jax.random.fold_in(own, 4), (amount // 2,), 0, 1 << 20) % (slack + 1)
    tallies = tallies.at[donor].add(-moved).at[taker].add(moved)
    labels = jnp.searchsorted(jnp.cumsum(tallies), jnp.arange(rows * top), side="right").astype(jnp.int32)
    table = labels.reshape(top, rows).T
    table = table[jax.random.permutation(jax.random.fold_in(own, 1), rows)]
    turn = jax.random.randint(jax.random.fold_in(own, 2), (rows, 1), 0, top)
    return jnp.take_along_axis(table, (jnp.arange(top)[None, :] + turn) % top, axis=1)


def load_shares(number_of, total, reach, lean, full):
    portions = [(1 << 20) // math.isqrt(standing ** lean) + 1 for standing in range(1, number_of + 1)]
    largest = reach if full else min(reach, max(-(-total // number_of), total * portions[0] // sum(portions)))
    least = 1 if total - largest >= number_of - 1 else 0
    given, rest = [largest] + [least] * (number_of - 1), total - largest - least * (number_of - 1)
    while rest > 0:
        candidates = [i for i in range(1, number_of) if given[i] < largest] or [i for i in range(1, number_of) if given[i] < reach]
        mass, remaining = sum([portions[i] for i in candidates]), rest
        for i in candidates:
            extra = min(reach - given[i], max(1, remaining * portions[i] // mass), rest)
            given[i] = given[i] + extra
            rest = rest - extra
    return np.array(given)


def scatter_about(rng, dims, spread, most, cuts=(), kind=jnp.bfloat16):
    entries = spread * jax.random.normal(rng, dims, jnp.float32)
    if cuts:
        entries = entries * levels(rng, dims, cuts, -0.22, 0.18)
    return jnp.clip(entries, -most, most).astype(kind)


def setup_inputs(seed: int = 0) -> dict:
    seeds = jax.random.split(jax.random.key(seed), 12)
    adjoint_guess = scatter_about(seeds[0], (2, L, NY, NX), 1.0, 6.0, ((1, 4), (2, 2), (3, 4)), jnp.float32)
    viscosity = jnp.clip(jnp.exp(math.log(2.0) - 2.3025851 * jax.random.uniform(seeds[1], (L, NY, NX), jnp.float32) ** levels(seeds[1], (L, NY, NX), ((0, 4), (1, 2), (2, 4)), -0.2, 0.2)), 0.2, 2.0)
    friction = jnp.clip(jnp.exp(math.log(5.0) - 3.218876 * jax.random.uniform(seeds[2], (NY, NX), jnp.float32) ** levels(seeds[2], (NY, NX), ((0, 2), (1, 4)), -0.2, 0.2)), 0.2, 5.0)
    base_velocity = scatter_about(seeds[3], (2, NY, NX), 1.0, 6.0, ((1, 2), (2, 4)), jnp.float32)
    surface_slope = scatter_about(seeds[4], (2, NY, NX), 1.0, 6.0, ((1, 2), (2, 4)), jnp.float32)
    ice_mask = plant((jax.random.randint(seeds[5], (NY, NX), 0, 5) < 4).astype(jnp.int32), jax.random.fold_in(seeds[5], 1), 0, 1)
    pixel_misfit = scatter_about(seeds[6], (ROWS,), 1.0, 6.0, ((0, 32),), jnp.float32)
    pixel_look = jnp.clip(jax.random.uniform(seeds[7], (ROWS,), jnp.float32, -3.140625, 3.140625), -3.140625, 3.140625)
    pixel_tile_keys = jax.random.split(jax.random.fold_in(seeds[8], 1), ROWS // ROWS_DEV)
    pixel_tile_turns = jax.random.permutation(jax.random.fold_in(seeds[8], 3), ROWS // ROWS_DEV)
    pixel_tile = jax.vmap(lambda own, number: assign_block(jax.random.fold_in(seeds[8], 2), own, number, ROWS_DEV, TILES, 1, CAP, 2))(pixel_tile_keys, pixel_tile_turns).reshape((ROWS, 1))
    pixel_cell = plant(jax.random.randint(seeds[9], (ROWS,), 0, CX * CY), jax.random.fold_in(seeds[9], 1), 0, (CX * CY) - 1).astype(jnp.int32)
    pixel_count = ragged_sizes(seeds[10], N_GX * N_GY * N_GZ, N_GX * N_GY * N_GZ * ROWS_DEV * 3 // 4, ROWS_DEV, 2).astype(jnp.int32)
    return dict(adjoint_guess=adjoint_guess, viscosity=viscosity, friction=friction, base_velocity=base_velocity, surface_slope=surface_slope, ice_mask=ice_mask, pixel_misfit=pixel_misfit, pixel_look=pixel_look, pixel_tile=pixel_tile, pixel_cell=pixel_cell, pixel_count=pixel_count)


OMEGA = 0.6
VERTICAL = 4.0


def box_apply(padded, visc_pad, mask_east, mask_north, mask_upper):
    first = padded[0]
    second = padded[1]
    base_a = first[:-1, :-1, :-1]
    base_b = second[:-1, :-1, :-1]
    east_a = (first[:-1, :-1, 1:] - base_a) * mask_east
    east_b = (second[:-1, :-1, 1:] - base_b) * mask_east
    north_a = (first[:-1, 1:, :-1] - base_a) * mask_north
    north_b = (second[:-1, 1:, :-1] - base_b) * mask_north
    upper_a = (first[1:, :-1, :-1] - base_a) * mask_upper
    upper_b = (second[1:, :-1, :-1] - base_b) * mask_upper
    visc_box = visc_pad[:-1, :-1, :-1]
    along_x = visc_box * (4.0 * east_a + 2.0 * north_b) * mask_east
    along_y = visc_box * (4.0 * north_b + 2.0 * east_a) * mask_north
    shear = visc_box * (north_a + east_b)
    shear_x = shear * mask_east
    shear_y = shear * mask_north
    vert_a = VERTICAL * visc_box * upper_a
    vert_b = VERTICAL * visc_box * upper_b
    result_a = (along_x[1:, 1:, :-1] - along_x[1:, 1:, 1:]) + (shear_y[1:, :-1, 1:] - shear_y[1:, 1:, 1:]) + (vert_a[:-1, 1:, 1:] - vert_a[1:, 1:, 1:])
    result_b = (along_y[1:, :-1, 1:] - along_y[1:, 1:, 1:]) + (shear_x[1:, 1:, :-1] - shear_x[1:, 1:, 1:]) + (vert_b[:-1, 1:, 1:] - vert_b[1:, 1:, 1:])
    return jnp.stack([result_a, result_b])


def reference(adjoint_guess, viscosity, friction, base_velocity, surface_slope, ice_mask, pixel_misfit, pixel_look, pixel_tile, pixel_cell, pixel_count):
    mask_float = ice_mask.astype(jnp.float32)
    row_ids = jnp.arange(ROWS, dtype=jnp.int32)
    device_ids = row_ids // ROWS_DEV
    live = (row_ids % ROWS_DEV) < pixel_count[device_ids]
    values = jnp.where(live, pixel_misfit, jnp.float32(0.0))
    force_x = values * jnp.cos(pixel_look)
    force_y = values * jnp.sin(pixel_look)
    tile_ids = pixel_tile[:, 0]
    col_x = (tile_ids // N_GY) * CX + pixel_cell % CX
    col_y = (tile_ids % N_GY) * CY + pixel_cell // CX
    forcing = jnp.zeros((2, NY, NX), jnp.float32)
    forcing = forcing.at[0, col_y, col_x].add(force_x).at[1, col_y, col_x].add(force_y)
    forcing = forcing * mask_float[None]
    layer_ids = jnp.arange(L, dtype=jnp.int32)
    bottom = (layer_ids == 0).astype(jnp.float32)[:, None, None]
    top = (layer_ids == L - 1).astype(jnp.float32)[:, None, None]
    rhs = forcing[:, None, :, :] * top[None]
    basal = friction[None] * bottom
    damping = OMEGA / (18.0 * viscosity + basal)
    east_ids = jnp.arange(NX + 1, dtype=jnp.int32) - 1
    north_ids = jnp.arange(NY + 1, dtype=jnp.int32) - 1
    upper_ids = jnp.arange(L + 1, dtype=jnp.int32) - 1
    mask_east = (east_ids + 1 < NX).astype(jnp.float32)[None, None, :]
    mask_north = (north_ids + 1 < NY).astype(jnp.float32)[None, :, None]
    mask_upper = (upper_ids + 1 < L).astype(jnp.float32)[:, None, None]
    visc_pad = jnp.pad(viscosity, 1)
    adjoint = adjoint_guess
    for sweep in range(ITERS):
        padded = jnp.pad(adjoint, ((0, 0), (1, 1), (1, 1), (1, 1)))
        image = box_apply(padded, visc_pad, mask_east, mask_north, mask_upper) + basal[None] * adjoint
        adjoint = adjoint + damping[None] * (rhs - image)
    fric_map = -mask_float * friction * (base_velocity[0] * adjoint[0, 0] + base_velocity[1] * adjoint[1, 0])
    drive_map = 0.25 * mask_float * jnp.sum(surface_slope[0][None] * adjoint[0] + surface_slope[1][None] * adjoint[1], axis=0)
    return adjoint, jnp.stack([fric_map, drive_map])
```

```python
import functools

import jax
import jax.numpy as jnp
from jax import lax
from jax.experimental import pallas as pl
from jax.experimental.pallas import tpu as pltpu
from jax.sharding import PartitionSpec as P

ITERS = 2


OMEGA = 0.6
VERTICAL = 4.0


def padded_2(block, sides, width):
    for axis, dim in sides:
        count = lax.axis_size(axis)
        forward = [(i, i + 1) for i in range(count - 1)]
        backward = [(target, source) for source, target in forward]
        low = lax.ppermute(
            lax.slice_in_dim(block, block.shape[dim] - width, None, axis=dim), axis, forward
        )
        high = lax.ppermute(lax.slice_in_dim(block, 0, width, axis=dim), axis, backward)
        block = jnp.concatenate([low, block, high], axis=dim)
    return block


def box_apply(padded, visc_pad, mask_east, mask_north, mask_upper):
    first = padded[0]
    second = padded[1]
    base_a = first[:-1, :-1, :-1]
    base_b = second[:-1, :-1, :-1]
    east_a = (first[:-1, :-1, 1:] - base_a) * mask_east
    east_b = (second[:-1, :-1, 1:] - base_b) * mask_east
    north_a = (first[:-1, 1:, :-1] - base_a) * mask_north
    north_b = (second[:-1, 1:, :-1] - base_b) * mask_north
    upper_a = (first[1:, :-1, :-1] - base_a) * mask_upper
    upper_b = (second[1:, :-1, :-1] - base_b) * mask_upper
    visc_box = visc_pad[:-1, :-1, :-1]
    along_x = visc_box * (4.0 * east_a + 2.0 * north_b) * mask_east
    along_y = visc_box * (4.0 * north_b + 2.0 * east_a) * mask_north
    shear = visc_box * (north_a + east_b)
    shear_x = shear * mask_east
    shear_y = shear * mask_north
    vert_a = VERTICAL * visc_box * upper_a
    vert_b = VERTICAL * visc_box * upper_b
    result_a = (
        along_x[1:, 1:, :-1]
        - along_x[1:, 1:, 1:]
        + (shear_y[1:, :-1, 1:] - shear_y[1:, 1:, 1:])
        + (vert_a[:-1, 1:, 1:] - vert_a[1:, 1:, 1:])
    )
    result_b = (
        along_y[1:, :-1, 1:]
        - along_y[1:, 1:, 1:]
        + (shear_x[1:, 1:, :-1] - shear_x[1:, 1:, 1:])
        + (vert_b[:-1, 1:, 1:] - vert_b[1:, 1:, 1:])
    )
    return jnp.stack([result_a, result_b])


def bin_kernel(tiles, rows, cols, fx_ref, fy_ref, tile_ref, cell_ref, out_ref, lhs, rhs):
    step = pl.program_id(0)
    depth = fx_ref.shape[1]
    tile = tile_ref[...]
    cell = cell_ref[...]
    col = lax.rem(cell, cols).astype(jnp.float32).astype(jnp.bfloat16)
    row = lax.div(cell, cols).astype(jnp.float32)
    fx = fx_ref[...]
    fy = fy_ref[...]
    fx_hi = fx.astype(jnp.bfloat16)
    fy_hi = fy.astype(jnp.bfloat16)
    fx_lo = (fx - fx_hi.astype(jnp.float32)).astype(jnp.bfloat16)
    fy_lo = (fy - fy_hi.astype(jnp.float32)).astype(jnp.bfloat16)
    x_ids = lax.broadcasted_iota(jnp.int32, (cols, depth), 0).astype(jnp.float32).astype(jnp.bfloat16)
    one = jnp.ones((cols, depth), jnp.bfloat16)
    rhs[...] = jnp.where(x_ids == col, one, jnp.zeros_like(one))
    y_ids = lax.broadcasted_iota(jnp.int32, (rows, depth), 0).astype(jnp.float32).astype(jnp.bfloat16)
    zero = jnp.zeros((rows, depth), jnp.bfloat16)
    for t in range(tiles):
        own = jnp.where(tile == t, row, -1.0).astype(jnp.bfloat16)
        hit = y_ids == own
        for c, piece in enumerate((fx_hi, fy_hi, fx_lo, fy_lo)):
            part = c // 2
            start = (t * 2 + c % 2) * rows
            lhs[part, start : start + rows, :] = jnp.where(hit, jnp.broadcast_to(piece, (rows, depth)), zero)
    total = lax.dot_general(
        lhs[0], rhs[...], (((1,), (1,)), ((), ())), preferred_element_type=jnp.float32
    ) + lax.dot_general(
        lhs[1], rhs[...], (((1,), (1,)), ((), ())), preferred_element_type=jnp.float32
    )

    @pl.when(step == 0)
    def _():
        out_ref[...] = total

    @pl.when(step > 0)
    def _():
        out_ref[...] += total


def bin_pixels(fx, fy, tile, cell, tiles, rows, cols):
    per_device = fx.shape[0]
    depth = min(1024, per_device)
    while depth * tiles * rows * 8 > 24 * 2**20:
        depth //= 2
    steps = per_device // depth
    flat = [value.reshape(steps, 1, depth) for value in (fx, fy, tile, cell)]
    spec = pl.BlockSpec((None, 1, depth), lambda i: (i, 0, 0))
    sums = pl.pallas_call(
        functools.partial(bin_kernel, tiles, rows, cols),
        grid=(steps,),
        in_specs=[spec] * 4,
        out_specs=pl.BlockSpec((tiles * 2 * rows, cols), lambda i: (0, 0)),
        out_shape=jax.ShapeDtypeStruct((tiles * 2 * rows, cols), jnp.float32),
        scratch_shapes=[
            pltpu.VMEM((2, tiles * 2 * rows, depth), jnp.bfloat16),
            pltpu.VMEM((cols, depth), jnp.bfloat16),
        ],
        name="bin_pixels",
    )(*flat)
    return sums.reshape(tiles, 2, rows, cols)


def body(
    adjoint_guess,
    viscosity,
    friction,
    base_velocity,
    surface_slope,
    ice_mask,
    pixel_misfit,
    pixel_look,
    pixel_tile,
    pixel_cell,
    pixel_count,
):
    layer_local = adjoint_guess.shape[1]
    rows_local = adjoint_guess.shape[2]
    cols_local = adjoint_guess.shape[3]
    count_x = lax.axis_size("gx")
    count_y = lax.axis_size("gy")
    count_z = lax.axis_size("gz")
    layer_total = layer_local * count_z
    full_x = cols_local * count_x
    full_y = rows_local * count_y
    tile_total = count_x * count_y
    per_device = pixel_misfit.shape[0]
    capacity = 2 * per_device // tile_total
    mask_float = ice_mask.astype(jnp.float32)
    live = jnp.arange(per_device, dtype=jnp.int32) < pixel_count[0]
    values = jnp.where(live, pixel_misfit, jnp.float32(0.0))
    sums = bin_pixels(
        values * jnp.cos(pixel_look),
        values * jnp.sin(pixel_look),
        pixel_tile[:, 0],
        pixel_cell,
        tile_total,
        rows_local,
        cols_local,
    )
    forcing = lax.psum_scatter(sums, ("gx", "gy"), scatter_dimension=0, tiled=True)
    forcing = forcing.reshape(2, rows_local, cols_local)
    forcing = lax.psum(forcing, "gz") * mask_float[None]
    layer_ids = lax.axis_index("gz") * layer_local + jnp.arange(layer_local, dtype=jnp.int32)
    bottom = (layer_ids == 0).astype(jnp.float32)[:, None, None]
    top = (layer_ids == layer_total - 1).astype(jnp.float32)[:, None, None]
    rhs = forcing[:, None, :, :] * top[None]
    basal = friction[None] * bottom
    damping = OMEGA / (18.0 * viscosity + basal)
    east_ids = lax.axis_index("gx") * cols_local + jnp.arange(cols_local + 1, dtype=jnp.int32) - 1
    north_ids = lax.axis_index("gy") * rows_local + jnp.arange(rows_local + 1, dtype=jnp.int32) - 1
    upper_ids = (
        lax.axis_index("gz") * layer_local + jnp.arange(layer_local + 1, dtype=jnp.int32) - 1
    )
    mask_east = (east_ids + 1 < full_x).astype(jnp.float32)[None, None, :]
    mask_north = (north_ids + 1 < full_y).astype(jnp.float32)[None, :, None]
    mask_upper = (upper_ids + 1 < layer_total).astype(jnp.float32)[:, None, None]
    adjoint = adjoint_guess
    for sweep in range(ITERS):
        stacked = jnp.concatenate([adjoint, viscosity[None]], axis=0)
        rims = padded_2(stacked, (("gx", 3), ("gy", 2), ("gz", 1)), 1)
        image = (
            box_apply(rims[:2], rims[2], mask_east, mask_north, mask_upper) + basal[None] * adjoint
        )
        adjoint = adjoint + damping[None] * (rhs - image)
    on_base = (lax.axis_index("gz") == 0).astype(jnp.float32)
    fric_term = (
        -on_base
        * mask_float
        * friction
        * (base_velocity[0] * adjoint[0, 0] + base_velocity[1] * adjoint[1, 0])
    )
    drive_term = (
        0.25
        * mask_float
        * jnp.sum(surface_slope[0][None] * adjoint[0] + surface_slope[1][None] * adjoint[1], axis=0)
    )
    maps = lax.psum_scatter(
        jnp.stack([fric_term, drive_term]), "gz", scatter_dimension=1, tiled=True
    )
    return (adjoint, maps)


def solution(mesh):
    return jax.shard_map(
        body,
        mesh=mesh,
        in_specs=(
            P(None, "gz", "gy", "gx"),
            P("gz", "gy", "gx"),
            P("gy", "gx"),
            P(None, "gy", "gx"),
            P(None, "gy", "gx"),
            P("gy", "gx"),
            P(("gx", "gy", "gz")),
            P(("gx", "gy", "gz")),
            P(("gx", "gy", "gz"), None),
            P(("gx", "gy", "gz")),
            P(("gx", "gy", "gz")),
        ),
        out_specs=(P(None, "gz", "gy", "gx"), P(None, ("gy", "gz"), "gx")),
        check_vma=False,
    )
```

```python
import functools

import jax
import jax.numpy as jnp
from jax import lax
from jax.experimental import pallas as pl
from jax.experimental.pallas import tpu as pltpu
from jax.sharding import PartitionSpec as P

ITERS = 2


OMEGA = 0.6
VERTICAL = 4.0


def bin_kernel(tiles, rows, cols, fx_ref, fy_ref, tile_ref, cell_ref, out_ref, lhs, rhs):
    step = pl.program_id(0)
    depth = fx_ref.shape[1]
    tile = tile_ref[...]
    cell = cell_ref[...]
    col = lax.rem(cell, cols).astype(jnp.float32).astype(jnp.bfloat16)
    row = lax.div(cell, cols).astype(jnp.float32)
    fx = fx_ref[...]
    fy = fy_ref[...]
    fx_hi = fx.astype(jnp.bfloat16)
    fy_hi = fy.astype(jnp.bfloat16)
    fx_lo = (fx - fx_hi.astype(jnp.float32)).astype(jnp.bfloat16)
    fy_lo = (fy - fy_hi.astype(jnp.float32)).astype(jnp.bfloat16)
    x_ids = lax.broadcasted_iota(jnp.int32, (cols, depth), 0).astype(jnp.float32).astype(jnp.bfloat16)
    one = jnp.ones((cols, depth), jnp.bfloat16)
    rhs[...] = jnp.where(x_ids == col, one, jnp.zeros_like(one))
    y_ids = lax.broadcasted_iota(jnp.int32, (rows, depth), 0).astype(jnp.float32).astype(jnp.bfloat16)
    zero = jnp.zeros((rows, depth), jnp.bfloat16)
    for t in range(tiles):
        own = jnp.where(tile == t, row, -1.0).astype(jnp.bfloat16)
        hit = y_ids == own
        for c, piece in enumerate((fx_hi, fy_hi, fx_lo, fy_lo)):
            part = c // 2
            start = (t * 2 + c % 2) * rows
            lhs[part, start : start + rows, :] = jnp.where(hit, jnp.broadcast_to(piece, (rows, depth)), zero)
    total = lax.dot_general(
        lhs[0], rhs[...], (((1,), (1,)), ((), ())), preferred_element_type=jnp.float32
    ) + lax.dot_general(
        lhs[1], rhs[...], (((1,), (1,)), ((), ())), preferred_element_type=jnp.float32
    )

    @pl.when(step == 0)
    def _():
        out_ref[...] = total

    @pl.when(step > 0)
    def _():
        out_ref[...] += total


def bin_pixels(fx, fy, tile, cell, tiles, rows, cols):
    per_device = fx.shape[0]
    depth = min(1024, per_device)
    while depth * tiles * rows * 8 > 24 * 2**20:
        depth //= 2
    steps = per_device // depth
    flat = [value.reshape(steps, 1, depth) for value in (fx, fy, tile, cell)]
    spec = pl.BlockSpec((None, 1, depth), lambda i: (i, 0, 0))
    sums = pl.pallas_call(
        functools.partial(bin_kernel, tiles, rows, cols),
        grid=(steps,),
        in_specs=[spec] * 4,
        out_specs=pl.BlockSpec((tiles * 2 * rows, cols), lambda i: (0, 0)),
        out_shape=jax.ShapeDtypeStruct((tiles * 2 * rows, cols), jnp.float32),
        scratch_shapes=[
            pltpu.VMEM((2, tiles * 2 * rows, depth), jnp.bfloat16),
            pltpu.VMEM((cols, depth), jnp.bfloat16),
        ],
        name="bin_pixels",
    )(*flat)
    return sums.reshape(tiles, 2, rows, cols)


def lane_column(pack, lane, like):
    return jnp.broadcast_to(pack[:, lane : lane + 1], like.shape)


def from_east(value, column):
    size = value.shape[1]
    lanes = lax.broadcasted_iota(jnp.int32, value.shape, 1)
    return jnp.where(lanes == size - 1, column, pltpu.roll(value, size - 1, 1))


def from_west(value, column):
    lanes = lax.broadcasted_iota(jnp.int32, value.shape, 1)
    return jnp.where(lanes == 0, column, pltpu.roll(value, 1, 1))


def from_north(value, row):
    size = value.shape[0]
    rows = lax.broadcasted_iota(jnp.int32, value.shape, 0)
    return jnp.where(rows == size - 1, row, pltpu.roll(value, size - 1, 0))


def from_south(value, row):
    rows = lax.broadcasted_iota(jnp.int32, value.shape, 0)
    return jnp.where(rows == 0, row, pltpu.roll(value, 1, 0))


def apply_kernel(
    counts,
    sums,
    guess,
    visc,
    fric,
    base,
    slope,
    mask,
    adj_out,
    maps_out,
    *scratch,
):
    nx, ny, nz = counts
    bits = nz.bit_length() - 1
    tiles = nx * ny
    layers, rows, cols = visc.shape
    scratch = list(scratch)
    accs = [scratch.pop(0) for _ in range(bits)]
    recvs = [scratch.pop(0) for _ in range(bits)]
    (
        tile_in,
        block,
        forcing,
        middle,
        west_edge,
        east_edge,
        south_edge,
        north_edge,
        halo_w,
        halo_e,
        halo_s,
        halo_n,
        halo_se,
        halo_nw,
        halo_d,
        halo_u,
        visc_d,
        part,
        part_in,
        half_sem,
        tile_sem,
        last_send,
        last_recv,
        halo_sem,
        visc_sem,
        part_sem,
    ) = scratch
    gx, gy, gz = lax.axis_index("gx"), lax.axis_index("gy"), lax.axis_index("gz")
    tile = gx * ny + gy
    lane_step = 16
    row_step = 8

    def remote(src, dst, send, recv, device):
        return pltpu.make_async_remote_copy(
            src_ref=src,
            dst_ref=dst,
            send_sem=send,
            recv_sem=recv,
            device_id=device,
            device_id_type=pl.DeviceIdType.MESH,
        )

    barrier = pltpu.get_barrier_semaphore()
    layer_peers = [(gx, gy, lax.rem(gz + o, nz)) for o in range(1, nz)]
    tile_peers = []
    for o in range(1, tiles):
        other = lax.rem(tile + o, tiles)
        tile_peers.append((other, (lax.div(other, ny), lax.rem(other, ny), gz)))
    for device in layer_peers + [device for _, device in tile_peers]:
        pl.semaphore_signal(barrier, inc=1, device_id=device, device_id_type=pl.DeviceIdType.MESH)
    pl.semaphore_wait(barrier, nz - 1 + tiles - 1)

    size = rows // 2
    starts = []
    offset = jnp.int32(0)
    for bit in range(bits):
        own_bit = lax.rem(lax.div(gz, 1 << bit), 2)
        keep = pl.multiple_of(own_bit * size, size)
        give = pl.multiple_of((1 - own_bit) * size, size)
        peer = (gx, gy, gz + (1 - 2 * own_bit) * (1 << bit))
        starts.append((keep, give, size, peer))
        offset = offset + own_bit * size
        size //= 2
    size = rows // nz
    offset = pl.multiple_of(offset, size)

    def half_copy(bit):
        _, give, length, peer = starts[bit]
        source = sums if bit == 0 else accs[bit - 1]
        return remote(
            source.at[:, :, pl.ds(give, length), :],
            recvs[bit],
            half_sem.at[0, bit],
            half_sem.at[1, bit],
            peer,
        )

    half_copy(0).start()

    def pack(field):
        lanes = lax.broadcasted_iota(jnp.int32, (rows, 128), 1)
        west = jnp.zeros((rows, 128), jnp.float32)
        east = jnp.zeros((rows, 128), jnp.float32)
        for f in range(3):
            for k in range(layers):
                value = field[f, k] if f < 2 else visc[k]
                south_edge[f * row_step + k : f * row_step + k + 1, :] = value[0:1, :]
                north_edge[f * row_step + k : f * row_step + k + 1, :] = value[rows - 1 : rows, :]
                lane = lanes == f * lane_step + k
                west = jnp.where(lane, lane_column(value, 0, west), west)
                east = jnp.where(lane, lane_column(value, cols - 1, east), east)
        west_edge[...] = west
        east_edge[...] = east

    def halo_copies(field, turn):
        def one(index, src, dst, device):
            return remote(src, dst, halo_sem.at[turn, 0, index], halo_sem.at[turn, 1, index], device)

        return [
            (one(0, west_edge, halo_e.at[turn], (gx - 1, gy, gz)), gx > 0, gx < nx - 1),
            (one(1, east_edge, halo_w.at[turn], (gx + 1, gy, gz)), gx < nx - 1, gx > 0),
            (one(2, south_edge, halo_n.at[turn], (gx, gy - 1, gz)), gy > 0, gy < ny - 1),
            (one(3, north_edge, halo_s.at[turn], (gx, gy + 1, gz)), gy < ny - 1, gy > 0),
            (
                one(4, north_edge.at[:, 0:128], halo_se.at[turn], (gx - 1, gy + 1, gz)),
                (gx > 0) & (gy < ny - 1),
                (gx < nx - 1) & (gy > 0),
            ),
            (
                one(5, east_edge.at[0:8, :], halo_nw.at[turn], (gx + 1, gy - 1, gz)),
                (gx < nx - 1) & (gy > 0),
                (gx > 0) & (gy < ny - 1),
            ),
            (one(6, field.at[:, 0], halo_u.at[turn], (gx, gy, gz - 1)), gz > 0, gz < nz - 1),
            (one(7, field.at[:, layers - 1], halo_d.at[turn], (gx, gy, gz + 1)), gz < nz - 1, gz > 0),
        ]

    def start_all(copies):
        for copy, sends, _ in copies:

            @pl.when(sends)
            def _(copy=copy):
                copy.start()

    def wait_all(copies):
        for copy, sends, receives in copies:

            @pl.when(receives)
            def _(copy=copy):
                copy.wait_recv()

            @pl.when(sends)
            def _(copy=copy):
                copy.wait_send()

    pack(guess)
    visc_up = (
        remote(visc.at[layers - 1], visc_d, visc_sem.at[0], visc_sem.at[1], (gx, gy, gz + 1)),
        gz < nz - 1,
        gz > 0,
    )
    first = halo_copies(guess, 0) + [visc_up]
    start_all(first)

    mask_float = mask[...].astype(jnp.float32)
    lane_ids = lax.broadcasted_iota(jnp.int32, (rows, cols), 1)
    row_ids = lax.broadcasted_iota(jnp.int32, (rows, cols), 0)
    mx = jnp.where((lane_ids < cols - 1) | (gx < nx - 1), 1.0, 0.0)
    my = jnp.where((row_ids < rows - 1) | (gy < ny - 1), 1.0, 0.0)
    my_col = my[:, 0:128]
    mx_row = mx[0:8, :]
    west_on = jnp.where(gx > 0, 1.0, 0.0)
    up_on = jnp.where(gz < nz - 1, 1.0, 0.0)

    def damping_of(k):
        scale = 18.0 * visc[k]
        if k == 0:
            scale = scale + jnp.where(gz == 0, fric[...], 0.0)
        return 0.6 / scale

    def sweep(field, turn, store):
        west = jnp.where(gx > 0, halo_w[turn], 0.0)
        east = jnp.where(gx < nx - 1, halo_e[turn], 0.0)
        south = jnp.where(gy > 0, halo_s[turn], 0.0)
        north = jnp.where(gy < ny - 1, halo_n[turn], 0.0)
        corner_se = jnp.where((gx < nx - 1) & (gy > 0), halo_se[turn], 0.0)
        corner_nw = jnp.where((gx > 0) & (gy < ny - 1), halo_nw[turn], 0.0)
        own_w = west_edge[...]
        own_s = south_edge[...]

        west_b = pltpu.roll(west, 128 - lane_step, 1)
        west_v = pltpu.roll(west, 128 - 2 * lane_step, 1)
        corner_b = pltpu.roll(corner_nw, 128 - lane_step, 1)
        col_na = (from_north(west, corner_nw[0:1, :]) - west) * my_col
        col_nb = (from_north(west_b, corner_b[0:1, :]) - west_b) * my_col
        col_ea = (own_w - west) * west_on
        col_eb = (pltpu.roll(own_w, 128 - lane_step, 1) - west_b) * west_on
        col_p = west_v * (4.0 * col_ea + 2.0 * col_nb) * west_on
        col_s = west_v * (col_na + col_eb) * west_on

        south_a, south_b, south_v = south[0:8], south[8:16], south[16:24]
        south_on = jnp.where(gy > 0, 1.0, 0.0)
        row_ea = (from_east(south_a, lane_column(corner_se[0:8], 0, south_a)) - south_a) * mx_row
        row_eb = (from_east(south_b, lane_column(corner_se[8:16], 0, south_b)) - south_b) * mx_row
        row_na = (own_s[0:8] - south_a) * south_on
        row_nb = (own_s[8:16] - south_b) * south_on
        row_q = south_v * (4.0 * row_nb + 2.0 * row_ea) * south_on
        row_s = south_v * (row_na + row_eb) * south_on

        below_v = jnp.where(gz > 0, visc_d[...], 0.0)
        low_a = 4.0 * below_v * (field[0, 0] - jnp.where(gz > 0, halo_d[turn, 0], 0.0))
        low_b = 4.0 * below_v * (field[1, 0] - jnp.where(gz > 0, halo_d[turn, 1], 0.0))
        for k in range(layers):
            va, vb, v = field[0, k], field[1, k], visc[k]
            ea = (from_east(va, lane_column(east, k, va)) - va) * mx
            eb = (from_east(vb, lane_column(east, lane_step + k, vb)) - vb) * mx
            na = (from_north(va, north[k : k + 1]) - va) * my
            nb = (from_north(vb, north[row_step + k : row_step + k + 1]) - vb) * my
            p = mx * v * (4.0 * ea + 2.0 * nb)
            q = my * v * (4.0 * nb + 2.0 * ea)
            s = v * (na + eb)
            sx = mx * s
            sy = my * s
            if k < layers - 1:
                top_a = 4.0 * v * (field[0, k + 1] - va)
                top_b = 4.0 * v * (field[1, k + 1] - vb)
            else:
                top_a = 4.0 * v * (jnp.where(gz < nz - 1, halo_u[turn, 0], 0.0) - va) * up_on
                top_b = 4.0 * v * (jnp.where(gz < nz - 1, halo_u[turn, 1], 0.0) - vb) * up_on
            image_a = (
                (from_west(p, lane_column(col_p, k, p)) - p)
                + (from_south(sy, row_s[k : k + 1]) - sy)
                + (low_a - top_a)
            )
            image_b = (
                (from_south(q, row_q[k : k + 1]) - q)
                + (from_west(sx, lane_column(col_s, k, sx)) - sx)
                + (low_b - top_b)
            )
            if k == 0:
                basal = jnp.where(gz == 0, fric[...], 0.0)
                image_a = image_a + basal * va
                image_b = image_b + basal * vb
            low_a, low_b = top_a, top_b
            damp = damping_of(k)
            store(k, va, vb, damp, image_a, image_b)

    def store_first(k, va, vb, damp, image_a, image_b):
        middle[0, k] = va - damp * image_a
        middle[1, k] = vb - damp * image_b

    for bit in range(bits):
        keep, give, length, _ = starts[bit]
        source = sums if bit == 0 else accs[bit - 1]
        copy = half_copy(bit)
        copy.wait_recv()
        if bit + 1 < bits:
            next_keep, next_give, next_length, _ = starts[bit + 1]
            for begin in (next_give, next_keep):
                accs[bit][:, :, pl.ds(begin, next_length), :] = (
                    source[:, :, pl.ds(pl.multiple_of(keep + begin, next_length), next_length), :]
                    + recvs[bit][:, :, pl.ds(begin, next_length), :]
                )
                if begin is next_give:
                    half_copy(bit + 1).start()
        else:
            accs[bit][...] = source[:, :, pl.ds(keep, length), :] + recvs[bit][...]
        if bit == bits - 2 or bits == 1:
            wait_all(first)
            sweep(guess, 0, store_first)
    total = accs[bits - 1]

    def tile_copy(o):
        other, device = tile_peers[o - 1]
        return remote(total.at[other], tile_in.at[o - 1], tile_sem.at[0, o - 1], tile_sem.at[1, o - 1], device)

    for o in range(1, tiles):
        tile_copy(o).start()
    value = total[tile]
    for o in range(1, tiles):
        tile_copy(o).wait_recv()
        value = value + tile_in[o - 1]
    block[...] = value

    def row_start(j):
        begin = 0
        length = rows // 2
        for bit in range(bits):
            begin += ((j >> bit) & 1) * length
            length //= 2
        return begin

    to_last = remote(
        block, forcing.at[:, pl.ds(offset, size), :], last_send, last_recv.at[gz], (gx, gy, nz - 1)
    )

    @pl.when(gz < nz - 1)
    def _():
        to_last.start()

    @pl.when(gz == nz - 1)
    def _():
        begin = row_start(nz - 1)
        forcing[:, begin : begin + size, :] = block[...]
        for j in range(nz - 1):
            begin = row_start(j)
            remote(
                block,
                forcing.at[:, begin : begin + size, :],
                last_send,
                last_recv.at[j],
                (gx, gy, 0),
            ).wait_recv()
        damp = damping_of(layers - 1)
        middle[0, layers - 1] = middle[0, layers - 1] + damp * (forcing[0] * mask_float)
        middle[1, layers - 1] = middle[1, layers - 1] + damp * (forcing[1] * mask_float)

    pack(middle)
    second = halo_copies(middle, 1)
    start_all(second)
    wait_all(second)

    on_base = jnp.where(gz == 0, 1.0, 0.0)
    drive = []

    def store_second(k, va, vb, damp, image_a, image_b):
        new_a = va - damp * image_a
        new_b = vb - damp * image_b
        if k == layers - 1:
            rhs_a = jnp.where(gz == nz - 1, forcing[0] * mask_float, 0.0)
            rhs_b = jnp.where(gz == nz - 1, forcing[1] * mask_float, 0.0)
            new_a = va + damp * (rhs_a - image_a)
            new_b = vb + damp * (rhs_b - image_b)
        adj_out[0, k] = new_a
        adj_out[1, k] = new_b
        term = slope[0] * new_a + slope[1] * new_b
        if k == 0:
            part[0] = -on_base * mask_float * fric[...] * (base[0] * new_a + base[1] * new_b)
            part[1] = term
        else:
            part[1] = part[1] + term

    sweep(middle, 1, store_second)
    part[1] = 0.25 * mask_float * part[1]

    def part_copy(o):
        device = layer_peers[o - 1]
        begin = pl.multiple_of(device[2] * size, size)
        return remote(
            part.at[:, pl.ds(begin, size), :],
            part_in.at[o - 1],
            part_sem.at[0, o - 1],
            part_sem.at[1, o - 1],
            device,
        )

    for o in range(1, nz):
        part_copy(o).start()
    value = part[:, pl.ds(pl.multiple_of(gz * size, size), size), :]
    for o in range(1, nz):
        part_copy(o).wait_recv()
        value = value + part_in[o - 1]
    maps_out[...] = value

    for bit in range(bits):
        half_copy(bit).wait_send()
    for o in range(1, tiles):
        tile_copy(o).wait_send()

    @pl.when(gz < nz - 1)
    def _():
        to_last.wait_send()

    for o in range(1, nz):
        part_copy(o).wait_send()


def apply_twice(sums, guess, visc, fric, base, slope, mask, counts):
    nx, ny, nz = counts
    tiles = nx * ny
    bits = nz.bit_length() - 1
    _, layers, rows, cols = guess.shape
    size = rows // nz
    f32 = jnp.float32
    halves = [pltpu.VMEM((tiles, 2, rows >> (bit + 1), cols), f32) for bit in range(bits)]
    vmem = pl.BlockSpec(memory_space=pltpu.VMEM)
    dma = pltpu.SemaphoreType.DMA
    return pl.pallas_call(
        functools.partial(apply_kernel, counts),
        in_specs=[vmem] * 7,
        out_specs=(vmem, vmem),
        out_shape=(
            jax.ShapeDtypeStruct(guess.shape, f32),
            jax.ShapeDtypeStruct((2, size, cols), f32),
        ),
        scratch_shapes=halves
        + halves
        + [
            pltpu.VMEM((tiles - 1, 2, size, cols), f32),
            pltpu.VMEM((2, size, cols), f32),
            pltpu.VMEM((2, rows, cols), f32),
            pltpu.VMEM(guess.shape, f32),
            pltpu.VMEM((rows, 128), f32),
            pltpu.VMEM((rows, 128), f32),
            pltpu.VMEM((24, cols), f32),
            pltpu.VMEM((24, cols), f32),
            pltpu.VMEM((2, rows, 128), f32),
            pltpu.VMEM((2, rows, 128), f32),
            pltpu.VMEM((2, 24, cols), f32),
            pltpu.VMEM((2, 24, cols), f32),
            pltpu.VMEM((2, 24, 128), f32),
            pltpu.VMEM((2, 8, 128), f32),
            pltpu.VMEM((2, 2, rows, cols), f32),
            pltpu.VMEM((2, 2, rows, cols), f32),
            pltpu.VMEM((rows, cols), f32),
            pltpu.VMEM((2, rows, cols), f32),
            pltpu.VMEM((nz - 1, 2, size, cols), f32),
            dma((2, bits)),
            dma((2, tiles - 1)),
            dma,
            dma((nz,)),
            dma((2, 2, 8)),
            dma((2,)),
            dma((2, nz - 1)),
        ],
        compiler_params=pltpu.CompilerParams(
            collective_id=0, has_side_effects=True, vmem_limit_bytes=56 * 2**20
        ),
        name="apply_twice",
    )(sums, guess, visc, fric, base, slope, mask)


def body(
    adjoint_guess,
    viscosity,
    friction,
    base_velocity,
    surface_slope,
    ice_mask,
    pixel_misfit,
    pixel_look,
    pixel_tile,
    pixel_cell,
    pixel_count,
):
    rows_local = adjoint_guess.shape[2]
    cols_local = adjoint_guess.shape[3]
    count_x = lax.axis_size("gx")
    count_y = lax.axis_size("gy")
    count_z = lax.axis_size("gz")
    tile_total = count_x * count_y
    per_device = pixel_misfit.shape[0]
    live = jnp.arange(per_device, dtype=jnp.int32) < pixel_count[0]
    values = jnp.where(live, pixel_misfit, jnp.float32(0.0))
    sums = bin_pixels(
        values * jnp.cos(pixel_look),
        values * jnp.sin(pixel_look),
        pixel_tile[:, 0],
        pixel_cell,
        tile_total,
        rows_local,
        cols_local,
    )
    return apply_twice(
        sums,
        adjoint_guess,
        viscosity,
        friction,
        base_velocity,
        surface_slope,
        ice_mask,
        (count_x, count_y, count_z),
    )


def solution(mesh):
    return jax.shard_map(
        body,
        mesh=mesh,
        in_specs=(
            P(None, "gz", "gy", "gx"),
            P("gz", "gy", "gx"),
            P("gy", "gx"),
            P(None, "gy", "gx"),
            P(None, "gy", "gx"),
            P("gy", "gx"),
            P(("gx", "gy", "gz")),
            P(("gx", "gy", "gz")),
            P(("gx", "gy", "gz"), None),
            P(("gx", "gy", "gz")),
            P(("gx", "gy", "gz")),
        ),
        out_specs=(P(None, "gz", "gy", "gx"), P(None, ("gy", "gz"), "gx")),
        check_vma=False,
    )
```

```python
import functools

import jax
import jax.numpy as jnp
from jax import lax
from jax.experimental import pallas as pl
from jax.experimental.pallas import tpu as pltpu
from jax.sharding import PartitionSpec as P

GROUPS = 4
DEPTH = 1024


def lane_column(pack, lane, like):
    return jnp.broadcast_to(pack[:, lane : lane + 1], like.shape)


def from_east(value, column):
    size = value.shape[1]
    lanes = lax.broadcasted_iota(jnp.int32, value.shape, 1)
    return jnp.where(lanes == size - 1, column, pltpu.roll(value, size - 1, 1))


def from_west(value, column):
    lanes = lax.broadcasted_iota(jnp.int32, value.shape, 1)
    return jnp.where(lanes == 0, column, pltpu.roll(value, 1, 1))


def from_north(value, row):
    size = value.shape[0]
    rows = lax.broadcasted_iota(jnp.int32, value.shape, 0)
    return jnp.where(rows == size - 1, row, pltpu.roll(value, size - 1, 0))


def from_south(value, row):
    rows = lax.broadcasted_iota(jnp.int32, value.shape, 0)
    return jnp.where(rows == 0, row, pltpu.roll(value, 1, 0))


def apply_kernel(
    counts,
    fx_ref,
    fy_ref,
    tile_ref,
    cell_ref,
    guess,
    visc,
    fric,
    base,
    slope,
    mask,
    adj_out,
    maps_out,
    *scratch,
):
    nx, ny, nz = counts
    bits = nz.bit_length() - 1
    tiles = nx * ny
    layers, rows, cols = visc.shape
    steps, _, depth = fx_ref.shape
    groups = GROUPS if tiles % GROUPS == 0 else 1
    per = tiles // groups
    scratch = list(scratch)
    accs = [scratch.pop(0) for _ in range(bits)]
    recvs = [scratch.pop(0) for _ in range(bits)]
    (
        sums,
        lhs,
        rhs,
        acc,
        tile_in,
        block,
        forcing,
        middle,
        west_edge,
        east_edge,
        south_edge,
        north_edge,
        halo_w,
        halo_e,
        halo_s,
        halo_n,
        halo_se,
        halo_nw,
        halo_d,
        halo_u,
        visc_d,
        part,
        part_in,
        half_sem,
        tile_sem,
        last_send,
        last_recv,
        halo_sem,
        visc_sem,
        part_sem,
    ) = scratch
    gx, gy, gz = lax.axis_index("gx"), lax.axis_index("gy"), lax.axis_index("gz")
    tile = gx * ny + gy
    lane_step = 16
    row_step = 8

    def remote(src, dst, send, recv, device):
        return pltpu.make_async_remote_copy(
            src_ref=src,
            dst_ref=dst,
            send_sem=send,
            recv_sem=recv,
            device_id=device,
            device_id_type=pl.DeviceIdType.MESH,
        )

    barrier = pltpu.get_barrier_semaphore()
    layer_peers = [(gx, gy, lax.rem(gz + o, nz)) for o in range(1, nz)]
    tile_peers = []
    for o in range(1, tiles):
        other = lax.rem(tile + o, tiles)
        tile_peers.append((other, (lax.div(other, ny), lax.rem(other, ny), gz)))
    for device in layer_peers + [device for _, device in tile_peers]:
        pl.semaphore_signal(barrier, inc=1, device_id=device, device_id_type=pl.DeviceIdType.MESH)
    pl.semaphore_wait(barrier, nz - 1 + tiles - 1)

    size = rows // 2
    starts = []
    offset = jnp.int32(0)
    for bit in range(bits):
        own_bit = lax.rem(lax.div(gz, 1 << bit), 2)
        keep = pl.multiple_of(own_bit * size, size)
        give = pl.multiple_of((1 - own_bit) * size, size)
        peer = (gx, gy, gz + (1 - 2 * own_bit) * (1 << bit))
        starts.append((keep, give, size, peer))
        offset = offset + own_bit * size
        size //= 2
    size = rows // nz
    offset = pl.multiple_of(offset, size)

    def half_copy(bit, g):
        _, give, length, peer = starts[bit]
        source = sums if bit == 0 else accs[bit - 1]
        own = pl.ds(g * per, per)
        return remote(
            source.at[own, :, pl.ds(give, length), :],
            recvs[bit].at[own],
            half_sem.at[0, bit, g],
            half_sem.at[1, bit, g],
            peer,
        )

    def bin_group(g):
        acc[...] = jnp.zeros_like(acc)

        def step(i, carry):
            tile_id = tile_ref[i]
            cell = cell_ref[i]
            row = lax.div(cell, cols).astype(jnp.float32)
            if g == 0:
                ids = lax.broadcasted_iota(jnp.int32, (cols, depth), 0)
                ids = ids.astype(jnp.float32).astype(jnp.bfloat16)
                col = lax.rem(cell, cols).astype(jnp.float32).astype(jnp.bfloat16)
                one = jnp.ones((cols, depth), jnp.bfloat16)
                rhs[i] = jnp.where(ids == col, one, jnp.zeros_like(one))
            pieces = []
            for value in (fx_ref[i], fy_ref[i]):
                high = value.astype(jnp.bfloat16)
                low = (value - high.astype(jnp.float32)).astype(jnp.bfloat16)
                pieces.append((high, low))
            ids = lax.broadcasted_iota(jnp.int32, (rows, depth), 0)
            ids = ids.astype(jnp.float32).astype(jnp.bfloat16)
            zero = jnp.zeros((rows, depth), jnp.bfloat16)
            for n in range(per):
                own = jnp.where(tile_id == g * per + n, row, -1.0).astype(jnp.bfloat16)
                hit = ids == own
                for c in range(2):
                    for part_id in range(2):
                        start = ((part_id * per + n) * 2 + c) * rows
                        piece = jnp.broadcast_to(pieces[c][part_id], (rows, depth))
                        lhs[start : start + rows, :] = jnp.where(hit, piece, zero)
            acc[...] += lax.dot_general(
                lhs[...], rhs[i], (((1,), (1,)), ((), ())), preferred_element_type=jnp.float32
            )
            return carry

        lax.fori_loop(0, steps, step, 0)
        half = per * 2 * rows
        sums[g * per : (g + 1) * per] = (acc[0:half] + acc[half : 2 * half]).reshape(
            per, 2, rows, cols
        )

    def pack(field):
        lanes = lax.broadcasted_iota(jnp.int32, (rows, 128), 1)
        west = jnp.zeros((rows, 128), jnp.float32)
        east = jnp.zeros((rows, 128), jnp.float32)
        for f in range(3):
            for k in range(layers):
                value = field[f, k] if f < 2 else visc[k]
                south_edge[f * row_step + k : f * row_step + k + 1, :] = value[0:1, :]
                north_edge[f * row_step + k : f * row_step + k + 1, :] = value[rows - 1 : rows, :]
                lane = lanes == f * lane_step + k
                west = jnp.where(lane, lane_column(value, 0, west), west)
                east = jnp.where(lane, lane_column(value, cols - 1, east), east)
        west_edge[...] = west
        east_edge[...] = east

    def halo_copies(field, turn):
        def one(index, src, dst, device):
            return remote(src, dst, halo_sem.at[turn, 0, index], halo_sem.at[turn, 1, index], device)

        return [
            (one(0, west_edge, halo_e.at[turn], (gx - 1, gy, gz)), gx > 0, gx < nx - 1),
            (one(1, east_edge, halo_w.at[turn], (gx + 1, gy, gz)), gx < nx - 1, gx > 0),
            (one(2, south_edge, halo_n.at[turn], (gx, gy - 1, gz)), gy > 0, gy < ny - 1),
            (one(3, north_edge, halo_s.at[turn], (gx, gy + 1, gz)), gy < ny - 1, gy > 0),
            (
                one(4, north_edge.at[:, 0:128], halo_se.at[turn], (gx - 1, gy + 1, gz)),
                (gx > 0) & (gy < ny - 1),
                (gx < nx - 1) & (gy > 0),
            ),
            (
                one(5, east_edge.at[0:8, :], halo_nw.at[turn], (gx + 1, gy - 1, gz)),
                (gx < nx - 1) & (gy > 0),
                (gx > 0) & (gy < ny - 1),
            ),
            (one(6, field.at[:, 0], halo_u.at[turn], (gx, gy, gz - 1)), gz > 0, gz < nz - 1),
            (one(7, field.at[:, layers - 1], halo_d.at[turn], (gx, gy, gz + 1)), gz < nz - 1, gz > 0),
        ]

    def start_all(copies):
        for copy, sends, _ in copies:

            @pl.when(sends)
            def _(copy=copy):
                copy.start()

    def wait_all(copies):
        for copy, sends, receives in copies:

            @pl.when(receives)
            def _(copy=copy):
                copy.wait_recv()

            @pl.when(sends)
            def _(copy=copy):
                copy.wait_send()

    pack(guess)
    visc_up = (
        remote(visc.at[layers - 1], visc_d, visc_sem.at[0], visc_sem.at[1], (gx, gy, gz + 1)),
        gz < nz - 1,
        gz > 0,
    )
    first = halo_copies(guess, 0) + [visc_up]
    start_all(first)

    mask_float = mask[...].astype(jnp.float32)
    lane_ids = lax.broadcasted_iota(jnp.int32, (rows, cols), 1)
    row_ids = lax.broadcasted_iota(jnp.int32, (rows, cols), 0)
    mx = jnp.where((lane_ids < cols - 1) | (gx < nx - 1), 1.0, 0.0)
    my = jnp.where((row_ids < rows - 1) | (gy < ny - 1), 1.0, 0.0)
    my_col = my[:, 0:128]
    mx_row = mx[0:8, :]
    west_on = jnp.where(gx > 0, 1.0, 0.0)
    up_on = jnp.where(gz < nz - 1, 1.0, 0.0)

    def damping_of(k):
        scale = 18.0 * visc[k]
        if k == 0:
            scale = scale + jnp.where(gz == 0, fric[...], 0.0)
        return 0.6 / scale

    def sweep(field, turn, store):
        west = jnp.where(gx > 0, halo_w[turn], 0.0)
        east = jnp.where(gx < nx - 1, halo_e[turn], 0.0)
        south = jnp.where(gy > 0, halo_s[turn], 0.0)
        north = jnp.where(gy < ny - 1, halo_n[turn], 0.0)
        corner_se = jnp.where((gx < nx - 1) & (gy > 0), halo_se[turn], 0.0)
        corner_nw = jnp.where((gx > 0) & (gy < ny - 1), halo_nw[turn], 0.0)
        own_w = west_edge[...]
        own_s = south_edge[...]

        west_b = pltpu.roll(west, 128 - lane_step, 1)
        west_v = pltpu.roll(west, 128 - 2 * lane_step, 1)
        corner_b = pltpu.roll(corner_nw, 128 - lane_step, 1)
        col_na = (from_north(west, corner_nw[0:1, :]) - west) * my_col
        col_nb = (from_north(west_b, corner_b[0:1, :]) - west_b) * my_col
        col_ea = (own_w - west) * west_on
        col_eb = (pltpu.roll(own_w, 128 - lane_step, 1) - west_b) * west_on
        col_p = west_v * (4.0 * col_ea + 2.0 * col_nb) * west_on
        col_s = west_v * (col_na + col_eb) * west_on

        south_a, south_b, south_v = south[0:8], south[8:16], south[16:24]
        south_on = jnp.where(gy > 0, 1.0, 0.0)
        row_ea = (from_east(south_a, lane_column(corner_se[0:8], 0, south_a)) - south_a) * mx_row
        row_eb = (from_east(south_b, lane_column(corner_se[8:16], 0, south_b)) - south_b) * mx_row
        row_na = (own_s[0:8] - south_a) * south_on
        row_nb = (own_s[8:16] - south_b) * south_on
        row_q = south_v * (4.0 * row_nb + 2.0 * row_ea) * south_on
        row_s = south_v * (row_na + row_eb) * south_on

        below_v = jnp.where(gz > 0, visc_d[...], 0.0)
        low_a = 4.0 * below_v * (field[0, 0] - jnp.where(gz > 0, halo_d[turn, 0], 0.0))
        low_b = 4.0 * below_v * (field[1, 0] - jnp.where(gz > 0, halo_d[turn, 1], 0.0))
        for k in range(layers):
            va, vb, v = field[0, k], field[1, k], visc[k]
            ea = (from_east(va, lane_column(east, k, va)) - va) * mx
            eb = (from_east(vb, lane_column(east, lane_step + k, vb)) - vb) * mx
            na = (from_north(va, north[k : k + 1]) - va) * my
            nb = (from_north(vb, north[row_step + k : row_step + k + 1]) - vb) * my
            p = mx * v * (4.0 * ea + 2.0 * nb)
            q = my * v * (4.0 * nb + 2.0 * ea)
            s = v * (na + eb)
            sx = mx * s
            sy = my * s
            if k < layers - 1:
                top_a = 4.0 * v * (field[0, k + 1] - va)
                top_b = 4.0 * v * (field[1, k + 1] - vb)
            else:
                top_a = 4.0 * v * (jnp.where(gz < nz - 1, halo_u[turn, 0], 0.0) - va) * up_on
                top_b = 4.0 * v * (jnp.where(gz < nz - 1, halo_u[turn, 1], 0.0) - vb) * up_on
            image_a = (
                (from_west(p, lane_column(col_p, k, p)) - p)
                + (from_south(sy, row_s[k : k + 1]) - sy)
                + (low_a - top_a)
            )
            image_b = (
                (from_south(q, row_q[k : k + 1]) - q)
                + (from_west(sx, lane_column(col_s, k, sx)) - sx)
                + (low_b - top_b)
            )
            if k == 0:
                basal = jnp.where(gz == 0, fric[...], 0.0)
                image_a = image_a + basal * va
                image_b = image_b + basal * vb
            low_a, low_b = top_a, top_b
            damp = damping_of(k)
            store(k, va, vb, damp, image_a, image_b)
            yield k

    def store_first(k, va, vb, damp, image_a, image_b):
        middle[0, k] = va - damp * image_a
        middle[1, k] = vb - damp * image_b

    def tile_copy(t):
        device = (t // ny, t % ny, gz)
        return remote(
            total.at[t], tile_in.at[tile], tile_sem.at[0, t], tile_sem.at[1, tile], device
        )

    def finish(bit, g):
        keep, give, length, _ = starts[bit]
        source = sums if bit == 0 else accs[bit - 1]
        own = pl.ds(g * per, per)
        half_copy(bit, g).wait_recv()
        if bit + 1 < bits:
            next_keep, next_give, next_length, _ = starts[bit + 1]
            for begin in (next_give, next_keep):
                accs[bit][own, :, pl.ds(begin, next_length), :] = (
                    source[own, :, pl.ds(pl.multiple_of(keep + begin, next_length), next_length), :]
                    + recvs[bit][own, :, pl.ds(begin, next_length), :]
                )
                if begin is next_give:
                    half_copy(bit + 1, g).start()
            return
        accs[bit][own] = source[own, :, pl.ds(keep, length), :] + recvs[bit][own]
        for t in range(g * per, (g + 1) * per):

            @pl.when(tile != t)
            def _(t=t):
                tile_copy(t).start()

            @pl.when(tile == t)
            def _(t=t):
                tile_in[t] = total[t]

    total = accs[bits - 1]
    first_sweep = None
    for turn in range(groups + bits):
        if turn < groups:
            bin_group(turn)
            half_copy(0, turn).start()
        elif turn == groups:
            wait_all(first)
            first_sweep = sweep(guess, 0, store_first)
            for _ in range(2):
                next(first_sweep, None)
        else:
            for _ in range(2):
                next(first_sweep, None)
        for bit in reversed(range(bits)):
            g = turn - 1 - bit
            if 0 <= g < groups:
                finish(bit, g)
    for _ in first_sweep:
        pass
    for t in range(tiles):

        @pl.when(tile != t)
        def _(t=t):
            remote(
                total.at[t], tile_in.at[t], tile_sem.at[0, t], tile_sem.at[1, t], (t // ny, t % ny, gz)
            ).wait_recv()

    value = tile_in[0]
    for t in range(1, tiles):
        value = value + tile_in[t]
    block[...] = value

    def row_start(j):
        begin = 0
        length = rows // 2
        for bit in range(bits):
            begin += ((j >> bit) & 1) * length
            length //= 2
        return begin

    to_last = remote(
        block, forcing.at[:, pl.ds(offset, size), :], last_send, last_recv.at[gz], (gx, gy, nz - 1)
    )

    @pl.when(gz < nz - 1)
    def _():
        to_last.start()

    @pl.when(gz == nz - 1)
    def _():
        begin = row_start(nz - 1)
        forcing[:, begin : begin + size, :] = block[...]
        for j in range(nz - 1):
            begin = row_start(j)
            remote(
                block,
                forcing.at[:, begin : begin + size, :],
                last_send,
                last_recv.at[j],
                (gx, gy, 0),
            ).wait_recv()
        damp = damping_of(layers - 1)
        middle[0, layers - 1] = middle[0, layers - 1] + damp * (forcing[0] * mask_float)
        middle[1, layers - 1] = middle[1, layers - 1] + damp * (forcing[1] * mask_float)

    pack(middle)
    second = halo_copies(middle, 1)
    start_all(second)
    wait_all(second)

    on_base = jnp.where(gz == 0, 1.0, 0.0)
    drive = []

    def store_second(k, va, vb, damp, image_a, image_b):
        new_a = va - damp * image_a
        new_b = vb - damp * image_b
        if k == layers - 1:
            rhs_a = jnp.where(gz == nz - 1, forcing[0] * mask_float, 0.0)
            rhs_b = jnp.where(gz == nz - 1, forcing[1] * mask_float, 0.0)
            new_a = va + damp * (rhs_a - image_a)
            new_b = vb + damp * (rhs_b - image_b)
        adj_out[0, k] = new_a
        adj_out[1, k] = new_b
        term = slope[0] * new_a + slope[1] * new_b
        if k == 0:
            part[0] = -on_base * mask_float * fric[...] * (base[0] * new_a + base[1] * new_b)
            part[1] = term
        else:
            part[1] = part[1] + term

    for _ in sweep(middle, 1, store_second):
        pass
    part[1] = 0.25 * mask_float * part[1]

    def part_copy(o):
        device = layer_peers[o - 1]
        begin = pl.multiple_of(device[2] * size, size)
        return remote(
            part.at[:, pl.ds(begin, size), :],
            part_in.at[o - 1],
            part_sem.at[0, o - 1],
            part_sem.at[1, o - 1],
            device,
        )

    for o in range(1, nz):
        part_copy(o).start()
    value = part[:, pl.ds(pl.multiple_of(gz * size, size), size), :]
    for o in range(1, nz):
        part_copy(o).wait_recv()
        value = value + part_in[o - 1]
    maps_out[...] = value

    for bit in range(bits):
        for g in range(groups):
            half_copy(bit, g).wait_send()
    for t in range(tiles):

        @pl.when(tile != t)
        def _(t=t):
            tile_copy(t).wait_send()

    @pl.when(gz < nz - 1)
    def _():
        to_last.wait_send()

    for o in range(1, nz):
        part_copy(o).wait_send()


def apply_twice(pixels, guess, visc, fric, base, slope, mask, counts):
    nx, ny, nz = counts
    tiles = nx * ny
    bits = nz.bit_length() - 1
    _, layers, rows, cols = guess.shape
    size = rows // nz
    f32 = jnp.float32
    groups = GROUPS if tiles % GROUPS == 0 else 1
    per = tiles // groups
    per_device = pixels[0].shape[0]
    depth = min(DEPTH, per_device)
    steps = per_device // depth
    flat = [value.reshape(steps, 1, depth) for value in pixels]
    halves = [pltpu.VMEM((tiles, 2, rows >> (bit + 1), cols), f32) for bit in range(bits)]
    vmem = pl.BlockSpec(memory_space=pltpu.VMEM)
    dma = pltpu.SemaphoreType.DMA
    return pl.pallas_call(
        functools.partial(apply_kernel, counts),
        in_specs=[vmem] * 10,
        out_specs=(vmem, vmem),
        out_shape=(
            jax.ShapeDtypeStruct(guess.shape, f32),
            jax.ShapeDtypeStruct((2, size, cols), f32),
        ),
        scratch_shapes=halves
        + halves
        + [
            pltpu.VMEM((tiles, 2, rows, cols), f32),
            pltpu.VMEM((per * 4 * rows, depth), jnp.bfloat16),
            pltpu.VMEM((steps, cols, depth), jnp.bfloat16),
            pltpu.VMEM((per * 4 * rows, cols), f32),
            pltpu.VMEM((tiles, 2, size, cols), f32),
            pltpu.VMEM((2, size, cols), f32),
            pltpu.VMEM((2, rows, cols), f32),
            pltpu.VMEM(guess.shape, f32),
            pltpu.VMEM((rows, 128), f32),
            pltpu.VMEM((rows, 128), f32),
            pltpu.VMEM((24, cols), f32),
            pltpu.VMEM((24, cols), f32),
            pltpu.VMEM((2, rows, 128), f32),
            pltpu.VMEM((2, rows, 128), f32),
            pltpu.VMEM((2, 24, cols), f32),
            pltpu.VMEM((2, 24, cols), f32),
            pltpu.VMEM((2, 24, 128), f32),
            pltpu.VMEM((2, 8, 128), f32),
            pltpu.VMEM((2, 2, rows, cols), f32),
            pltpu.VMEM((2, 2, rows, cols), f32),
            pltpu.VMEM((rows, cols), f32),
            pltpu.VMEM((2, rows, cols), f32),
            pltpu.VMEM((nz - 1, 2, size, cols), f32),
            dma((2, bits, groups)),
            dma((2, tiles)),
            dma,
            dma((nz,)),
            dma((2, 2, 8)),
            dma((2,)),
            dma((2, nz - 1)),
        ],
        compiler_params=pltpu.CompilerParams(
            collective_id=0, has_side_effects=True, vmem_limit_bytes=56 * 2**20
        ),
        name="apply_twice",
    )(*flat, guess, visc, fric, base, slope, mask)


def body(
    adjoint_guess,
    viscosity,
    friction,
    base_velocity,
    surface_slope,
    ice_mask,
    pixel_misfit,
    pixel_look,
    pixel_tile,
    pixel_cell,
    pixel_count,
):
    count_x = lax.axis_size("gx")
    count_y = lax.axis_size("gy")
    count_z = lax.axis_size("gz")
    per_device = pixel_misfit.shape[0]
    live = jnp.arange(per_device, dtype=jnp.int32) < pixel_count[0]
    values = jnp.where(live, pixel_misfit, jnp.float32(0.0))
    pixels = (
        values * jnp.cos(pixel_look),
        values * jnp.sin(pixel_look),
        pixel_tile[:, 0],
        pixel_cell,
    )
    return apply_twice(
        pixels,
        adjoint_guess,
        viscosity,
        friction,
        base_velocity,
        surface_slope,
        ice_mask,
        (count_x, count_y, count_z),
    )


def solution(mesh):
    return jax.shard_map(
        body,
        mesh=mesh,
        in_specs=(
            P(None, "gz", "gy", "gx"),
            P("gz", "gy", "gx"),
            P("gy", "gx"),
            P(None, "gy", "gx"),
            P(None, "gy", "gx"),
            P("gy", "gx"),
            P(("gx", "gy", "gz")),
            P(("gx", "gy", "gz")),
            P(("gx", "gy", "gz"), None),
            P(("gx", "gy", "gz")),
            P(("gx", "gy", "gz")),
        ),
        out_specs=(P(None, "gz", "gy", "gx"), P(None, ("gy", "gz"), "gx")),
        check_vma=False,
    )
```

```python
import functools
import math

import jax
import jax.numpy as jnp
from jax import lax
from jax.experimental import pallas as pl
from jax.experimental.pallas import tpu as pltpu
from jax.sharding import PartitionSpec as P

GROUPS = 4
SLOT_TILES = 8
DEPTH = 1024


def lane_column(pack, lane, like):
    return jnp.broadcast_to(pack[:, lane : lane + 1], like.shape)


def from_east(value, column):
    size = value.shape[1]
    lanes = lax.broadcasted_iota(jnp.int32, value.shape, 1)
    return jnp.where(lanes == size - 1, column, pltpu.roll(value, size - 1, 1))


def from_west(value, column):
    lanes = lax.broadcasted_iota(jnp.int32, value.shape, 1)
    return jnp.where(lanes == 0, column, pltpu.roll(value, 1, 1))


def from_north(value, row):
    size = value.shape[0]
    rows = lax.broadcasted_iota(jnp.int32, value.shape, 0)
    return jnp.where(rows == size - 1, row, pltpu.roll(value, size - 1, 0))


def from_south(value, row):
    rows = lax.broadcasted_iota(jnp.int32, value.shape, 0)
    return jnp.where(rows == 0, row, pltpu.roll(value, 1, 0))


def apply_kernel(
    counts,
    fx_ref,
    fy_ref,
    tile_ref,
    cell_ref,
    guess,
    visc,
    fric,
    base,
    slope,
    mask,
    adj_out,
    maps_out,
    *scratch,
):
    nx, ny, nz = counts
    bits = nz.bit_length() - 1
    tiles = nx * ny
    layers, rows, cols = visc.shape
    steps, _, depth = fx_ref.shape
    groups = GROUPS if tiles % GROUPS == 0 else 1
    per = tiles // groups
    scratch = list(scratch)
    accs = [scratch.pop(0) for _ in range(bits)]
    recvs = [scratch.pop(0) for _ in range(bits)]
    (
        sums,
        lhs,
        rhs,
        acc,
        tile_in,
        block,
        forcing,
        middle,
        west_edge,
        east_edge,
        south_edge,
        north_edge,
        halo_w,
        halo_e,
        halo_s,
        halo_n,
        halo_se,
        halo_nw,
        halo_d,
        halo_u,
        visc_d,
        part,
        part_in,
        half_sem,
        tile_sem,
        last_send,
        last_recv,
        halo_sem,
        visc_sem,
        part_sem,
    ) = scratch
    gx, gy, gz = lax.axis_index("gx"), lax.axis_index("gy"), lax.axis_index("gz")
    tile = gx * ny + gy
    lane_step = 16
    row_step = 8

    def remote(src, dst, send, recv, device):
        return pltpu.make_async_remote_copy(
            src_ref=src,
            dst_ref=dst,
            send_sem=send,
            recv_sem=recv,
            device_id=device,
            device_id_type=pl.DeviceIdType.MESH,
        )

    barrier = pltpu.get_barrier_semaphore()
    layer_peers = [(gx, gy, lax.rem(gz + o, nz)) for o in range(1, nz)]
    tile_peers = []
    for o in range(1, tiles):
        other = lax.rem(tile + o, tiles)
        tile_peers.append((other, (lax.div(other, ny), lax.rem(other, ny), gz)))
    for device in layer_peers + [device for _, device in tile_peers]:
        pl.semaphore_signal(barrier, inc=1, device_id=device, device_id_type=pl.DeviceIdType.MESH)
    pl.semaphore_wait(barrier, nz - 1 + tiles - 1)

    size = rows // 2
    starts = []
    offset = jnp.int32(0)
    for bit in range(bits):
        own_bit = lax.rem(lax.div(gz, 1 << bit), 2)
        keep = pl.multiple_of(own_bit * size, size)
        give = pl.multiple_of((1 - own_bit) * size, size)
        peer = (gx, gy, gz + (1 - 2 * own_bit) * (1 << bit))
        starts.append((keep, give, size, peer))
        offset = offset + own_bit * size
        size //= 2
    size = rows // nz
    offset = pl.multiple_of(offset, size)

    def half_copy(bit, g):
        _, give, length, peer = starts[bit]
        source = sums if bit == 0 else accs[bit - 1]
        own = pl.ds(g * per, per)
        return remote(
            source.at[own, :, pl.ds(give, length), :],
            recvs[bit].at[own],
            half_sem.at[0, bit, g],
            half_sem.at[1, bit, g],
            peer,
        )

    def bin_group(g):
        acc[...] = jnp.zeros_like(acc)

        def step(i, slot):
            tile_id = tile_ref[i]
            cell = cell_ref[i]
            row = lax.div(cell, cols).astype(jnp.float32)
            if g == 0:
                ids = lax.broadcasted_iota(jnp.int32, (cols, depth), 0)
                ids = ids.astype(jnp.float32).astype(jnp.bfloat16)
                col = lax.rem(cell, cols).astype(jnp.float32).astype(jnp.bfloat16)
                one = jnp.ones((cols, depth), jnp.bfloat16)
                rhs[i] = jnp.where(ids == col, one, jnp.zeros_like(one))
            pieces = []
            for value in (fx_ref[i], fy_ref[i]):
                high = value.astype(jnp.bfloat16)
                low = (value - high.astype(jnp.float32)).astype(jnp.bfloat16)
                pieces.append((high, low))
            ids = lax.broadcasted_iota(jnp.int32, (rows, depth), 0)
            ids = ids.astype(jnp.float32).astype(jnp.bfloat16)
            zero = jnp.zeros((rows, depth), jnp.bfloat16)
            for n in range(per):
                own = jnp.where(tile_id == g * per + n, row, -1.0).astype(jnp.bfloat16)
                hit = ids == own
                for c in range(2):
                    for part_id in range(2):
                        start = ((part_id * per + n) * 2 + c) * rows
                        piece = jnp.broadcast_to(pieces[c][part_id], (rows, depth))
                        lhs[slot, start : start + rows, :] = jnp.where(hit, piece, zero)
            acc[...] += lax.dot_general(
                lhs[slot], rhs[i], (((1,), (1,)), ((), ())), preferred_element_type=jnp.float32
            )

        def several(j, carry):
            for slot in range(unroll):
                step(j * unroll + slot, slot)
            return carry

        unroll = lhs.shape[0]
        lax.fori_loop(0, steps // unroll, several, 0)
        half = per * 2 * rows
        sums[g * per : (g + 1) * per] = (acc[0:half] + acc[half : 2 * half]).reshape(
            per, 2, rows, cols
        )

    def pack(field):
        lanes = lax.broadcasted_iota(jnp.int32, (rows, 128), 1)
        west = jnp.zeros((rows, 128), jnp.float32)
        east = jnp.zeros((rows, 128), jnp.float32)
        for f in range(3):
            for k in range(layers):
                value = field[f, k] if f < 2 else visc[k]
                south_edge[f * row_step + k : f * row_step + k + 1, :] = value[0:1, :]
                north_edge[f * row_step + k : f * row_step + k + 1, :] = value[rows - 1 : rows, :]
                lane = lanes == f * lane_step + k
                west = jnp.where(lane, lane_column(value, 0, west), west)
                east = jnp.where(lane, lane_column(value, cols - 1, east), east)
        west_edge[...] = west
        east_edge[...] = east

    def halo_copies(field, turn):
        def one(index, src, dst, device):
            return remote(src, dst, halo_sem.at[turn, 0, index], halo_sem.at[turn, 1, index], device)

        return [
            (one(0, west_edge, halo_e.at[turn], (gx - 1, gy, gz)), gx > 0, gx < nx - 1),
            (one(1, east_edge, halo_w.at[turn], (gx + 1, gy, gz)), gx < nx - 1, gx > 0),
            (one(2, south_edge, halo_n.at[turn], (gx, gy - 1, gz)), gy > 0, gy < ny - 1),
            (one(3, north_edge, halo_s.at[turn], (gx, gy + 1, gz)), gy < ny - 1, gy > 0),
            (
                one(4, north_edge.at[:, 0:128], halo_se.at[turn], (gx - 1, gy + 1, gz)),
                (gx > 0) & (gy < ny - 1),
                (gx < nx - 1) & (gy > 0),
            ),
            (
                one(5, east_edge.at[0:8, :], halo_nw.at[turn], (gx + 1, gy - 1, gz)),
                (gx < nx - 1) & (gy > 0),
                (gx > 0) & (gy < ny - 1),
            ),
            (one(6, field.at[:, 0], halo_u.at[turn], (gx, gy, gz - 1)), gz > 0, gz < nz - 1),
            (one(7, field.at[:, layers - 1], halo_d.at[turn], (gx, gy, gz + 1)), gz < nz - 1, gz > 0),
        ]

    def start_all(copies):
        for copy, sends, _ in copies:

            @pl.when(sends)
            def _(copy=copy):
                copy.start()

    def wait_all(copies):
        for copy, sends, receives in copies:

            @pl.when(receives)
            def _(copy=copy):
                copy.wait_recv()

            @pl.when(sends)
            def _(copy=copy):
                copy.wait_send()

    pack(guess)
    visc_up = (
        remote(visc.at[layers - 1], visc_d, visc_sem.at[0], visc_sem.at[1], (gx, gy, gz + 1)),
        gz < nz - 1,
        gz > 0,
    )
    first = halo_copies(guess, 0) + [visc_up]
    start_all(first)

    mask_float = mask[...].astype(jnp.float32)
    lane_ids = lax.broadcasted_iota(jnp.int32, (rows, cols), 1)
    row_ids = lax.broadcasted_iota(jnp.int32, (rows, cols), 0)
    mx = jnp.where((lane_ids < cols - 1) | (gx < nx - 1), 1.0, 0.0)
    my = jnp.where((row_ids < rows - 1) | (gy < ny - 1), 1.0, 0.0)
    my_col = my[:, 0:128]
    mx_row = mx[0:8, :]
    west_on = jnp.where(gx > 0, 1.0, 0.0)
    up_on = jnp.where(gz < nz - 1, 1.0, 0.0)

    def damping_of(k):
        scale = 18.0 * visc[k]
        if k == 0:
            scale = scale + jnp.where(gz == 0, fric[...], 0.0)
        return 0.6 / scale

    def sweep(field, turn, store):
        west = jnp.where(gx > 0, halo_w[turn], 0.0)
        east = jnp.where(gx < nx - 1, halo_e[turn], 0.0)
        south = jnp.where(gy > 0, halo_s[turn], 0.0)
        north = jnp.where(gy < ny - 1, halo_n[turn], 0.0)
        corner_se = jnp.where((gx < nx - 1) & (gy > 0), halo_se[turn], 0.0)
        corner_nw = jnp.where((gx > 0) & (gy < ny - 1), halo_nw[turn], 0.0)
        own_w = west_edge[...]
        own_s = south_edge[...]

        west_b = pltpu.roll(west, 128 - lane_step, 1)
        west_v = pltpu.roll(west, 128 - 2 * lane_step, 1)
        corner_b = pltpu.roll(corner_nw, 128 - lane_step, 1)
        col_na = (from_north(west, corner_nw[0:1, :]) - west) * my_col
        col_nb = (from_north(west_b, corner_b[0:1, :]) - west_b) * my_col
        col_ea = (own_w - west) * west_on
        col_eb = (pltpu.roll(own_w, 128 - lane_step, 1) - west_b) * west_on
        col_p = west_v * (4.0 * col_ea + 2.0 * col_nb) * west_on
        col_s = west_v * (col_na + col_eb) * west_on

        south_a, south_b, south_v = south[0:8], south[8:16], south[16:24]
        south_on = jnp.where(gy > 0, 1.0, 0.0)
        row_ea = (from_east(south_a, lane_column(corner_se[0:8], 0, south_a)) - south_a) * mx_row
        row_eb = (from_east(south_b, lane_column(corner_se[8:16], 0, south_b)) - south_b) * mx_row
        row_na = (own_s[0:8] - south_a) * south_on
        row_nb = (own_s[8:16] - south_b) * south_on
        row_q = south_v * (4.0 * row_nb + 2.0 * row_ea) * south_on
        row_s = south_v * (row_na + row_eb) * south_on

        below_v = jnp.where(gz > 0, visc_d[...], 0.0)
        low_a = 4.0 * below_v * (field[0, 0] - jnp.where(gz > 0, halo_d[turn, 0], 0.0))
        low_b = 4.0 * below_v * (field[1, 0] - jnp.where(gz > 0, halo_d[turn, 1], 0.0))
        for k in range(layers):
            va, vb, v = field[0, k], field[1, k], visc[k]
            ea = (from_east(va, lane_column(east, k, va)) - va) * mx
            eb = (from_east(vb, lane_column(east, lane_step + k, vb)) - vb) * mx
            na = (from_north(va, north[k : k + 1]) - va) * my
            nb = (from_north(vb, north[row_step + k : row_step + k + 1]) - vb) * my
            p = mx * v * (4.0 * ea + 2.0 * nb)
            q = my * v * (4.0 * nb + 2.0 * ea)
            s = v * (na + eb)
            sx = mx * s
            sy = my * s
            if k < layers - 1:
                top_a = 4.0 * v * (field[0, k + 1] - va)
                top_b = 4.0 * v * (field[1, k + 1] - vb)
            else:
                top_a = 4.0 * v * (jnp.where(gz < nz - 1, halo_u[turn, 0], 0.0) - va) * up_on
                top_b = 4.0 * v * (jnp.where(gz < nz - 1, halo_u[turn, 1], 0.0) - vb) * up_on
            image_a = (
                (from_west(p, lane_column(col_p, k, p)) - p)
                + (from_south(sy, row_s[k : k + 1]) - sy)
                + (low_a - top_a)
            )
            image_b = (
                (from_south(q, row_q[k : k + 1]) - q)
                + (from_west(sx, lane_column(col_s, k, sx)) - sx)
                + (low_b - top_b)
            )
            if k == 0:
                basal = jnp.where(gz == 0, fric[...], 0.0)
                image_a = image_a + basal * va
                image_b = image_b + basal * vb
            low_a, low_b = top_a, top_b
            damp = damping_of(k)
            store(k, va, vb, damp, image_a, image_b)
            yield k

    def store_first(k, va, vb, damp, image_a, image_b):
        middle[0, k] = va - damp * image_a
        middle[1, k] = vb - damp * image_b

    def tile_copy(t):
        device = (t // ny, t % ny, gz)
        return remote(
            total.at[t], tile_in.at[tile], tile_sem.at[0, t], tile_sem.at[1, tile], device
        )

    def finish(bit, g):
        keep, give, length, _ = starts[bit]
        source = sums if bit == 0 else accs[bit - 1]
        own = pl.ds(g * per, per)
        half_copy(bit, g).wait_recv()
        if bit + 1 < bits:
            next_keep, next_give, next_length, _ = starts[bit + 1]
            for begin in (next_give, next_keep):
                accs[bit][own, :, pl.ds(begin, next_length), :] = (
                    source[own, :, pl.ds(pl.multiple_of(keep + begin, next_length), next_length), :]
                    + recvs[bit][own, :, pl.ds(begin, next_length), :]
                )
                if begin is next_give:
                    half_copy(bit + 1, g).start()
            return
        accs[bit][own] = source[own, :, pl.ds(keep, length), :] + recvs[bit][own]
        for t in range(g * per, (g + 1) * per):

            @pl.when(tile != t)
            def _(t=t):
                tile_copy(t).start()

            @pl.when(tile == t)
            def _(t=t):
                tile_in[t] = total[t]

    total = accs[bits - 1]
    first_sweep = None
    for turn in range(groups + bits):
        if turn < groups:
            bin_group(turn)
            half_copy(0, turn).start()
        elif turn == groups:
            wait_all(first)
            first_sweep = sweep(guess, 0, store_first)
            for _ in range(2):
                next(first_sweep, None)
        else:
            for _ in range(2):
                next(first_sweep, None)
        for bit in reversed(range(bits)):
            g = turn - 1 - bit
            if 0 <= g < groups:
                finish(bit, g)
    for _ in first_sweep:
        pass
    for t in range(tiles):

        @pl.when(tile != t)
        def _(t=t):
            remote(
                total.at[t], tile_in.at[t], tile_sem.at[0, t], tile_sem.at[1, t], (t // ny, t % ny, gz)
            ).wait_recv()

    value = tile_in[0]
    for t in range(1, tiles):
        value = value + tile_in[t]
    block[...] = value

    def row_start(j):
        begin = 0
        length = rows // 2
        for bit in range(bits):
            begin += ((j >> bit) & 1) * length
            length //= 2
        return begin

    to_last = remote(
        block, forcing.at[:, pl.ds(offset, size), :], last_send, last_recv.at[gz], (gx, gy, nz - 1)
    )

    @pl.when(gz < nz - 1)
    def _():
        to_last.start()

    @pl.when(gz == nz - 1)
    def _():
        begin = row_start(nz - 1)
        forcing[:, begin : begin + size, :] = block[...]
        for j in range(nz - 1):
            begin = row_start(j)
            remote(
                block,
                forcing.at[:, begin : begin + size, :],
                last_send,
                last_recv.at[j],
                (gx, gy, 0),
            ).wait_recv()
        damp = damping_of(layers - 1)
        middle[0, layers - 1] = middle[0, layers - 1] + damp * (forcing[0] * mask_float)
        middle[1, layers - 1] = middle[1, layers - 1] + damp * (forcing[1] * mask_float)

    pack(middle)
    second = halo_copies(middle, 1)
    start_all(second)
    wait_all(second)

    on_base = jnp.where(gz == 0, 1.0, 0.0)
    drive = []

    def store_second(k, va, vb, damp, image_a, image_b):
        new_a = va - damp * image_a
        new_b = vb - damp * image_b
        if k == layers - 1:
            rhs_a = jnp.where(gz == nz - 1, forcing[0] * mask_float, 0.0)
            rhs_b = jnp.where(gz == nz - 1, forcing[1] * mask_float, 0.0)
            new_a = va + damp * (rhs_a - image_a)
            new_b = vb + damp * (rhs_b - image_b)
        adj_out[0, k] = new_a
        adj_out[1, k] = new_b
        term = slope[0] * new_a + slope[1] * new_b
        if k == 0:
            part[0] = -on_base * mask_float * fric[...] * (base[0] * new_a + base[1] * new_b)
            part[1] = term
        else:
            part[1] = part[1] + term

    for _ in sweep(middle, 1, store_second):
        pass
    part[1] = 0.25 * mask_float * part[1]

    def part_copy(o):
        device = layer_peers[o - 1]
        begin = pl.multiple_of(device[2] * size, size)
        return remote(
            part.at[:, pl.ds(begin, size), :],
            part_in.at[o - 1],
            part_sem.at[0, o - 1],
            part_sem.at[1, o - 1],
            device,
        )

    for o in range(1, nz):
        part_copy(o).start()
    value = part[:, pl.ds(pl.multiple_of(gz * size, size), size), :]
    for o in range(1, nz):
        part_copy(o).wait_recv()
        value = value + part_in[o - 1]
    maps_out[...] = value

    for bit in range(bits):
        for g in range(groups):
            half_copy(bit, g).wait_send()
    for t in range(tiles):

        @pl.when(tile != t)
        def _(t=t):
            tile_copy(t).wait_send()

    @pl.when(gz < nz - 1)
    def _():
        to_last.wait_send()

    for o in range(1, nz):
        part_copy(o).wait_send()


def apply_twice(pixels, guess, visc, fric, base, slope, mask, counts):
    nx, ny, nz = counts
    tiles = nx * ny
    bits = nz.bit_length() - 1
    _, layers, rows, cols = guess.shape
    size = rows // nz
    f32 = jnp.float32
    groups = GROUPS if tiles % GROUPS == 0 else 1
    per = tiles // groups
    per_device = pixels[0].shape[0]
    depth = min(DEPTH, per_device)
    steps = per_device // depth
    flat = [value.reshape(steps, 1, depth) for value in pixels]
    slots = math.gcd(steps, max(1, SLOT_TILES // per))
    halves = [pltpu.VMEM((tiles, 2, rows >> (bit + 1), cols), f32) for bit in range(bits)]
    vmem = pl.BlockSpec(memory_space=pltpu.VMEM)
    dma = pltpu.SemaphoreType.DMA
    return pl.pallas_call(
        functools.partial(apply_kernel, counts),
        in_specs=[vmem] * 10,
        out_specs=(vmem, vmem),
        out_shape=(
            jax.ShapeDtypeStruct(guess.shape, f32),
            jax.ShapeDtypeStruct((2, size, cols), f32),
        ),
        scratch_shapes=halves
        + halves
        + [
            pltpu.VMEM((tiles, 2, rows, cols), f32),
            pltpu.VMEM((slots, per * 4 * rows, depth), jnp.bfloat16),
            pltpu.VMEM((steps, cols, depth), jnp.bfloat16),
            pltpu.VMEM((per * 4 * rows, cols), f32),
            pltpu.VMEM((tiles, 2, size, cols), f32),
            pltpu.VMEM((2, size, cols), f32),
            pltpu.VMEM((2, rows, cols), f32),
            pltpu.VMEM(guess.shape, f32),
            pltpu.VMEM((rows, 128), f32),
            pltpu.VMEM((rows, 128), f32),
            pltpu.VMEM((24, cols), f32),
            pltpu.VMEM((24, cols), f32),
            pltpu.VMEM((2, rows, 128), f32),
            pltpu.VMEM((2, rows, 128), f32),
            pltpu.VMEM((2, 24, cols), f32),
            pltpu.VMEM((2, 24, cols), f32),
            pltpu.VMEM((2, 24, 128), f32),
            pltpu.VMEM((2, 8, 128), f32),
            pltpu.VMEM((2, 2, rows, cols), f32),
            pltpu.VMEM((2, 2, rows, cols), f32),
            pltpu.VMEM((rows, cols), f32),
            pltpu.VMEM((2, rows, cols), f32),
            pltpu.VMEM((nz - 1, 2, size, cols), f32),
            dma((2, bits, groups)),
            dma((2, tiles)),
            dma,
            dma((nz,)),
            dma((2, 2, 8)),
            dma((2,)),
            dma((2, nz - 1)),
        ],
        compiler_params=pltpu.CompilerParams(
            collective_id=0, has_side_effects=True, vmem_limit_bytes=56 * 2**20
        ),
        name="apply_twice",
    )(*flat, guess, visc, fric, base, slope, mask)


def body(
    adjoint_guess,
    viscosity,
    friction,
    base_velocity,
    surface_slope,
    ice_mask,
    pixel_misfit,
    pixel_look,
    pixel_tile,
    pixel_cell,
    pixel_count,
):
    count_x = lax.axis_size("gx")
    count_y = lax.axis_size("gy")
    count_z = lax.axis_size("gz")
    per_device = pixel_misfit.shape[0]
    live = jnp.arange(per_device, dtype=jnp.int32) < pixel_count[0]
    values = jnp.where(live, pixel_misfit, jnp.float32(0.0))
    pixels = (
        values * jnp.cos(pixel_look),
        values * jnp.sin(pixel_look),
        pixel_tile[:, 0],
        pixel_cell,
    )
    return apply_twice(
        pixels,
        adjoint_guess,
        viscosity,
        friction,
        base_velocity,
        surface_slope,
        ice_mask,
        (count_x, count_y, count_z),
    )


def solution(mesh):
    return jax.shard_map(
        body,
        mesh=mesh,
        in_specs=(
            P(None, "gz", "gy", "gx"),
            P("gz", "gy", "gx"),
            P("gy", "gx"),
            P(None, "gy", "gx"),
            P(None, "gy", "gx"),
            P("gy", "gx"),
            P(("gx", "gy", "gz")),
            P(("gx", "gy", "gz")),
            P(("gx", "gy", "gz"), None),
            P(("gx", "gy", "gz")),
            P(("gx", "gy", "gz")),
        ),
        out_specs=(P(None, "gz", "gy", "gx"), P(None, ("gy", "gz"), "gx")),
        check_vma=False,
    )
```
